512 devices in a mesh: row: 32 (over x, z_hi, core), col: 16 (over z_lo, y).
Axes of the slice: x: 4, y: 4, z: 16 (z_hi: 4, z_lo: 4; z = z_hi * 4 + z_lo), core: 2. Of those that a mesh axis runs over, the one named last changes fastest.
Arguments:
- a_vals: bfloat16 [32, 16, 2, 6, 5, 128, 128], P('row', 'col'), may hold values from -6 to 6
- a_cols: int32 [32, 16, 2, 6, 5], P('row', 'col'), may hold values from 0 to 5, as said below
- b_vals: bfloat16 [32, 16, 6, 8, 128, 128], P('row', 'col'), may hold values from -0.15625 to 0.15625
- b_cols: int32 [32, 16, 6, 8], P('row', 'col'), may hold values from 0 to 11, as said below
- c_cols: int32 [32, 16, 6, 6], P('row', 'col'), may hold values from 0 to 11, as said below
- panel_owner: int32 [32, 32], replicated, may hold values from 0 to 31, as said below
- atom_size: int32 [192], replicated, may hold values from 64 to 128
Outputs:
- product_blocks: bfloat16 [32, 16, 6, 6, 128, 128], P('row', 'col')
The draws below stay inside these ranges and needn't reach their ends.
Inputs may be any that keep to these rules, and one draw needn't show every extreme that they name: `a_cols`: the 5 indices of one block row are distinct. `b_cols`: the 8 indices of one block row are distinct. `c_cols`: the 6 indices of one block row are distinct. `panel_owner`: each row is a permutation.
All inputs are finite; a program needn't handle non-finite values.
Results may differ from the reference program's by a relative error of at most 0.001.
Values may be sent and summed in bfloat16 or wider, within the bound.
A program may use at most 128 MiB of HBM per device.

```python
import jax
import jax.numpy as jnp
from jax import lax

BLK = 128
KB = 6
NZA = 5
NZB = 8
NCS = 6
STEPS = 2
CB = 12
NBLK = 192
N_ROW = 32
N_COL = 16


def distinct_picks(key, lead_shape, pool, count):
    raw = jax.random.randint(key, tuple(lead_shape) + (pool,), 0, 1 << 20)
    scores = raw * pool + jnp.arange(pool, dtype=jnp.int32)
    order = jnp.argsort(scores, axis=-1)
    return order[..., :count].astype(jnp.int32)


def draw_a_cols(key, part):
    return distinct_picks(jax.random.fold_in(key, 11), (N_ROW, N_COL, 2, KB), KB, NZA)


def draw_b_cols(key, part):
    return distinct_picks(jax.random.fold_in(key, 23), (N_ROW, N_COL, KB), 2 * KB, NZB)


def draw_c_cols(key, part):
    return distinct_picks(jax.random.fold_in(key, 37), (N_ROW, N_COL, KB), 2 * KB, NCS)


def draw_panel_owner(key, part):
    return distinct_picks(jax.random.fold_in(key, 41), (N_ROW,), N_ROW, N_ROW)


def set_ends(drawn, stream_key, least, largest):
    extent = drawn.shape
    place = [jax.random.randint(jax.random.fold_in(stream_key, axis), (), 0, extent[axis]) for axis in range(len(extent))]
    drawn = drawn.at[tuple(place)].set(least)
    longest = extent.index(max(extent))
    place[longest] = (place[longest] + 1) % extent[longest]
    return drawn.at[tuple(place)].set(largest)


def level_of(stream_key, dims, split, least, largest):
    def one(dim, blocks):
        draws = jax.random.uniform(jax.random.fold_in(jax.random.fold_in(stream_key, 6), dim), (blocks,), jnp.float32, least / len(split), largest / len(split))
        return jnp.repeat(jnp.exp(draws), dims[dim] // blocks).reshape((-1,) + (1,) * (len(dims) - dim - 1))

    gain = one(*split[0])
    for cut in split[1:]:
        gain = gain * one(*cut)
    return gain


def noise(rng, shape, width, bound, shards=(), kind=jnp.bfloat16):
    loudness = level_of(rng, shape, shards, -0.22, 0.18) if shards else 1.0
    values = jax.random.normal(rng, shape, jnp.float32) * width * loudness
    return jnp.minimum(jnp.maximum(values, -bound), bound).astype(kind)


def setup_inputs(seed: int = 0) -> dict:
    arg_keys = jax.random.split(jax.random.key(seed), 8)
    return {
        "a_vals": noise(arg_keys[0], (N_ROW, N_COL, 2, KB, NZA, BLK, BLK), 1.0, 6.0, ((0, 32), (1, 16))),
        "a_cols": draw_a_cols(jax.random.fold_in(arg_keys[7], 71), 0),
        "b_vals": noise(arg_keys[2], (N_ROW, N_COL, KB, NZB, BLK, BLK), (STEPS * NZA * BLK) ** -0.5, 0.15625, ((0, 32), (1, 16))),
        "b_cols": draw_b_cols(jax.random.fold_in(arg_keys[7], 71), 0),
        "c_cols": draw_c_cols(jax.random.fold_in(arg_keys[7], 71), 0),
        "panel_owner": draw_panel_owner(jax.random.fold_in(arg_keys[7], 71), 0),
        "atom_size": set_ends(jax.random.randint(arg_keys[6], (NBLK,), BLK // 2, BLK + 1), jax.random.fold_in(arg_keys[6], 1), BLK // 2, BLK).astype(jnp.int32),
    }


def sizes_at(atom_size, start, count):
    return lax.dynamic_slice_in_dim(atom_size, start, count)


def pick_sizes(indices, table):
    lane_ids = jnp.arange(table.shape[0], dtype=jnp.int32)
    return jnp.sum(jnp.where(indices[..., None] == lane_ids, table, 0), axis=-1)


def panel_term(avals, acols, bvals, bcols, ccols, k_sizes):
    block_size = avals.shape[-1]
    inner_sizes = pick_sizes(acols, k_sizes)
    inside = jnp.arange(block_size, dtype=jnp.int32) < inner_sizes[..., None]
    masked = jnp.where(inside[..., None, :], avals, jnp.zeros((), avals.dtype))
    picked_v = bvals[acols]
    picked_c = bcols[acols]
    products = jnp.einsum('imab,imnbc->imnac', masked.astype(jnp.float32), picked_v.astype(jnp.float32), precision=lax.Precision.HIGHEST)
    select = (picked_c[..., None] == ccols[:, None, None, :]).astype(jnp.float32)
    return jnp.einsum('imns,imnac->isac', select, products, precision=lax.Precision.HIGHEST)


def finish(summed, ccols, row_sizes, col_table):
    block_size = summed.shape[-1]
    col_sizes = pick_sizes(ccols, col_table)
    lane_ids = jnp.arange(block_size, dtype=jnp.int32)
    inside = (lane_ids[:, None] < row_sizes[:, None, None, None]) & (lane_ids[None, :] < col_sizes[:, :, None, None])
    return jnp.where(inside, summed, jnp.zeros((), summed.dtype)).astype(jnp.bfloat16)


def reference(a_vals, a_cols, b_vals, b_cols, c_cols, panel_owner, atom_size):
    def one_panel(flat_index):
        row_id = flat_index // N_COL
        col_id = flat_index % N_COL
        summed = jnp.zeros((KB, NCS, BLK, BLK), jnp.float32)
        for fox_step in range(STEPS):
            k_panel = (row_id + fox_step) % N_ROW
            position = panel_owner[row_id, k_panel]
            holder = position // 2
            slot_index = position % 2
            summed = summed + panel_term(a_vals[row_id, holder, slot_index], a_cols[row_id, holder, slot_index], b_vals[k_panel, col_id], b_cols[k_panel, col_id], c_cols[row_id, col_id], sizes_at(atom_size, k_panel * KB, KB))
        return finish(summed, c_cols[row_id, col_id], sizes_at(atom_size, row_id * KB, KB), sizes_at(atom_size, col_id * CB, CB))

    result = lax.map(one_panel, jnp.arange(N_ROW * N_COL, dtype=jnp.int32))
    return result.reshape(N_ROW, N_COL, KB, NCS, BLK, BLK)
```

```python
import functools

import jax
import jax.numpy as jnp
from jax import lax
from jax.experimental import pallas as pl
from jax.experimental.pallas import tpu as pltpu
from jax.sharding import PartitionSpec as P

MESH = pl.DeviceIdType.MESH
BLK = 128
KB = 6
NZA = 5
NZB = 8
NCS = 6
CB = 12
NY = 4
NZ = 4
ROWS = KB * NZA * BLK
SLICE = ROWS // NY
PER = 3
CH = SLICE // PER
HF = CH // 2
NCHUNK = 2 * PER
PIECE = 3
NPIECE = KB * NZB // PIECE


def remote(src, dst, send_sem, recv_sem, device):
    return pltpu.make_async_remote_copy(
        src_ref=src, dst_ref=dst, send_sem=send_sem, recv_sem=recv_sem,
        device_id=device, device_id_type=MESH)


def move_kernel(n_row, n_col, owner_ref, a_ref, ac_ref, b_ref, bc_ref,
                out_ref, acg_ref, bn_ref, bcn_ref,
                sel, r_up, r_dn, r_opp, l_up, l_dn, t_buf, u_in, d_in, u_out, d_out, full,
                s_y1, v_y1, s_z, v_z, s_y2, v_y2, s_b, v_b, s_i, v_i, loc):
    me_r = lax.axis_index("row")
    me_c = lax.axis_index("col")
    y = lax.rem(me_c, NY)
    q = me_c // NY
    y_p = lax.rem(y + 1, NY)
    y_m = lax.rem(y + NY - 1, NY)
    y_o = lax.rem(y + 2, NY)
    dev_p = (me_r, q * NY + y_p)
    dev_m = (me_r, q * NY + y_m)
    dev_u = (me_r, lax.rem(me_c + NY, n_col))
    dev_d = (me_r, lax.rem(me_c + n_col - NY, n_col))
    to_b = (lax.rem(me_r + n_row - 1, n_row), me_c)
    from_b = (lax.rem(me_r + 1, n_row), me_c)

    barrier = pltpu.get_barrier_semaphore()
    for d in range(1, n_col):
        pl.semaphore_signal(barrier, inc=1, device_id=(me_r, lax.rem(me_c + d, n_col)), device_id_type=MESH)
    pl.semaphore_signal(barrier, inc=1, device_id=to_b, device_id_type=MESH)
    pl.semaphore_signal(barrier, inc=1, device_id=from_b, device_id_type=MESH)

    for s in range(2):
        place = owner_ref[me_r, lax.rem(me_r + s, n_row)]
        f0 = (place == 2 * me_c).astype(jnp.float32).astype(jnp.bfloat16)
        f1 = (place == 2 * me_c + 1).astype(jnp.float32).astype(jnp.bfloat16)

        @pl.loop(0, ROWS // HF)
        def _(g):
            at = pl.ds(pl.multiple_of(g * HF, HF), HF)
            sel[s, at, :] = a_ref[0, at, :] * f0 + a_ref[1, at, :] * f1

    pl.semaphore_wait(barrier, n_col + 1)

    own_ac = pltpu.make_async_copy(ac_ref, acg_ref.at[me_c], loc.at[0])
    own_ac.start()
    idx = []
    for d in range(1, n_col):
        cp = remote(ac_ref, acg_ref.at[me_c], s_i.at[d], v_i.at[d], (me_r, lax.rem(me_c + d, n_col)))
        cp.start()
        idx.append(cp)
    cp = remote(bc_ref, bcn_ref, s_i.at[0], v_i.at[0], to_b)
    cp.start()
    idx.append(cp)

    pieces = []

    def piece():
        k = len(pieces)
        if k < NPIECE:
            at = pl.ds(k * PIECE, PIECE)
            cp = remote(b_ref.at[at], bn_ref.at[at], s_b.at[k], v_b.at[k], to_b)
            cp.start()
            pieces.append(cp)

    def rows_of(slice_id, c, off, size):
        return pl.ds(pl.multiple_of(slice_id * SLICE + (c % PER) * CH + off, 16), size)

    def y1(c):
        s = c // PER
        return (
            remote(sel.at[s, rows_of(y_o, c, 0, HF)], l_up.at[c], s_y1.at[c, 0], v_y1.at[c, 0], dev_p),
            remote(sel.at[s, rows_of(y_o, c, HF, HF)], l_dn.at[c], s_y1.at[c, 1], v_y1.at[c, 1], dev_m),
            remote(sel.at[s, rows_of(y_p, c, 0, CH)], r_up.at[c], s_y1.at[c, 2], v_y1.at[c, 2], dev_p),
            remote(sel.at[s, rows_of(y_m, c, 0, CH)], r_dn.at[c], s_y1.at[c, 3], v_y1.at[c, 3], dev_m),
            remote(l_up.at[c], r_opp.at[c, pl.ds(0, HF)], s_y1.at[c, 4], v_y1.at[c, 4], dev_p),
            remote(l_dn.at[c], r_opp.at[c, pl.ds(HF, HF)], s_y1.at[c, 5], v_y1.at[c, 5], dev_m),
        )

    y1s = [y1(c) for c in range(NCHUNK)]

    def first(c):
        for cp in y1s[c][:4]:
            cp.start()

    def relay(c):
        y1s[c][0].wait_recv()
        y1s[c][4].start()
        y1s[c][1].wait_recv()
        y1s[c][5].start()

    def zs(c):
        return (
            remote(u_out.at[c], u_in.at[c], s_z.at[c, 0], v_z.at[c, 0], dev_u),
            remote(d_out.at[c], d_in.at[c], s_z.at[c, 1], v_z.at[c, 1], dev_d),
        )

    zss = [zs(c) for c in range(NCHUNK)]

    def gather_slice(c):
        s = c // PER
        for j in (2, 3, 4, 5):
            y1s[c][j].wait_recv()
        t = sel[s, rows_of(y, c, 0, CH), :] + r_up[c] + r_dn[c] + r_opp[c]
        t_buf[c] = t

        @pl.when(q == 0)
        def _():
            u_out[c] = t
            zss[c][0].start()

        @pl.when(q == NZ - 1)
        def _():
            d_out[c] = t
            zss[c][1].start()

    def y2(c):
        s = c // PER
        own = rows_of(y, c, 0, CH)
        lo = rows_of(y_m, c, 0, HF)
        hi = rows_of(y_p, c, HF, HF)
        return (
            remote(full.at[s, own], full.at[s, own], s_y2.at[c, 0], v_y2.at[c, 0], dev_p),
            remote(full.at[s, own], full.at[s, own], s_y2.at[c, 1], v_y2.at[c, 1], dev_m),
            remote(full.at[s, lo], full.at[s, lo], s_y2.at[c, 2], v_y2.at[c, 2], dev_p),
            remote(full.at[s, hi], full.at[s, hi], s_y2.at[c, 3], v_y2.at[c, 3], dev_m),
        )

    y2s = [y2(c) for c in range(NCHUNK)]

    def chain(c):
        s = c // PER

        @pl.when(q > 0)
        def _():
            zss[c][0].wait_recv()
            u_out[c] = t_buf[c] + u_in[c]

        @pl.when((q > 0) & (q < NZ - 1))
        def _():
            zss[c][0].start()

        @pl.when(q < NZ - 1)
        def _():
            zss[c][1].wait_recv()
            d_out[c] = t_buf[c] + d_in[c]

        @pl.when((q > 0) & (q < NZ - 1))
        def _():
            zss[c][1].start()

        own = rows_of(y, c, 0, CH)

        @pl.when(q < NZ - 1)
        def _():
            full[s, own, :] = u_out[c] + d_in[c]

        @pl.when(q == NZ - 1)
        def _():
            full[s, own, :] = u_out[c]

        y2s[c][0].start()
        y2s[c][1].start()

    def pass_on(c):
        y2s[c][0].wait_recv()
        y2s[c][2].start()
        y2s[c][1].wait_recv()
        y2s[c][3].start()

    first(0)
    first(1)
    piece()
    piece()
    for c in range(NCHUNK + 3):
        if c < NCHUNK:
            relay(c)
        if c + 2 < NCHUNK:
            first(c + 2)
        piece()
        if 0 <= c - 2 < NCHUNK:
            chain(c - 2)
        if 0 <= c - 3 < NCHUNK:
            pass_on(c - 3)
        piece()
        if c < NCHUNK:
            gather_slice(c)
    while len(pieces) < NPIECE:
        piece()
    outs = []
    for s in range(2):
        for c in range(s * PER, (s + 1) * PER):
            y2s[c][2].wait_recv()
            y2s[c][3].wait_recv()
        cp = pltpu.make_async_copy(full.at[s], out_ref.at[s], loc.at[1 + s])
        cp.start()
        outs.append(cp)
    for c in range(NCHUNK):
        for cp in y1s[c]:
            cp.wait_send()
        for cp in y2s[c]:
            cp.wait_send()

        @pl.when(q < NZ - 1)
        def _():
            zss[c][0].wait_send()

        @pl.when(q > 0)
        def _():
            zss[c][1].wait_send()

    own_ac.wait()
    for cp in idx + pieces + outs:
        cp.wait()


def compute_kernel(n_row, owner_ref, size_ref, acg_ref, bc_ref, bcn_ref, cc_ref, a_ref, b_ref, bn_ref, o_ref,
                   table, bbuf, lhs, rhs, sem):
    me_r = lax.axis_index("row")
    me_c = lax.axis_index("col")
    nb = KB * NZB
    loads = []
    for s, ref in enumerate((b_ref, bn_ref)):
        cp = pltpu.make_async_copy(ref, bbuf.at[pl.ds(s * nb, nb)], sem.at[s])
        cp.start()
        loads.append(cp)
    bbuf[2 * nb] = jnp.zeros((BLK, BLK), jnp.bfloat16)
    for s, ref in enumerate((bc_ref, bcn_ref)):
        base = s * KB * CB

        @pl.loop(0, KB * CB)
        def _(e):
            table[base + e] = 2 * nb

        for j in range(KB):
            for n in range(NZB):
                table[base + j * CB + ref[j, n]] = s * nb + j * NZB + n
    roots = []
    for s in range(2):
        place = owner_ref[me_r, lax.rem(me_r + s, n_row)]
        roots.append((place // 2, lax.rem(place, 2), lax.rem(me_r + s, n_row) * KB))
    for cp in loads:
        cp.wait()
    lane = lax.broadcasted_iota(jnp.int32, (BLK, BLK), 1)
    line = lax.broadcasted_iota(jnp.int32, (BLK, BLK), 0)

    @pl.loop(0, KB)
    def _(i):
        for s in range(2):
            holder, slot, first = roots[s]
            for m in range(NZA):
                j = acg_ref[holder, slot, i, m]
                width = size_ref[first + j]
                at = (s * NZA + m) * BLK
                block = a_ref[s, i * NZA + m]
                lhs[:, pl.ds(at, BLK)] = jnp.where(lane < width, block, jnp.zeros((), jnp.bfloat16))
                for t in range(NCS):
                    where = table[s * KB * CB + j * CB + cc_ref[i, t]]
                    rhs[pl.ds(at, BLK), pl.ds(t * BLK, BLK)] = bbuf[where]
        acc = jnp.dot(lhs[...], rhs[...], preferred_element_type=jnp.float32)
        height = size_ref[me_r * KB + i]
        for t in range(NCS):
            wide = size_ref[me_c * CB + cc_ref[i, t]]
            inside = (line < height) & (lane < wide)
            o_ref[i, t] = jnp.where(inside, acc[:, t * BLK:(t + 1) * BLK], 0.0).astype(jnp.bfloat16)


def local(n_row, n_col, a_vals, a_cols, b_vals, b_cols, c_cols, panel_owner, atom_size):
    a = a_vals.reshape(2, ROWS, BLK)
    ac = a_cols.reshape(2, KB, NZA)
    b = b_vals.reshape(KB * NZB, BLK, BLK)
    bc = b_cols.reshape(KB, NZB)
    cc = c_cols.reshape(KB, NCS)
    any_ = pl.BlockSpec(memory_space=pl.ANY)
    vmem = pl.BlockSpec(memory_space=pltpu.VMEM)
    smem = pl.BlockSpec(memory_space=pltpu.SMEM)
    bf = jnp.bfloat16
    dma = pltpu.SemaphoreType.DMA
    panels, acg, bn, bcn = pl.pallas_call(
        functools.partial(move_kernel, n_row, n_col),
        out_shape=(
            jax.ShapeDtypeStruct((2, ROWS, BLK), bf),
            jax.ShapeDtypeStruct((n_col, 2, KB, NZA), jnp.int32),
            jax.ShapeDtypeStruct((KB * NZB, BLK, BLK), bf),
            jax.ShapeDtypeStruct((KB, NZB), jnp.int32),
        ),
        in_specs=[smem, vmem, any_, any_, any_],
        out_specs=(any_, any_, any_, any_),
        scratch_shapes=[
            pltpu.VMEM((2, ROWS, BLK), bf),
            pltpu.VMEM((NCHUNK, CH, BLK), bf),
            pltpu.VMEM((NCHUNK, CH, BLK), bf),
            pltpu.VMEM((NCHUNK, CH, BLK), bf),
            pltpu.VMEM((NCHUNK, HF, BLK), bf),
            pltpu.VMEM((NCHUNK, HF, BLK), bf),
            pltpu.VMEM((NCHUNK, CH, BLK), bf),
            pltpu.VMEM((NCHUNK, CH, BLK), bf),
            pltpu.VMEM((NCHUNK, CH, BLK), bf),
            pltpu.VMEM((NCHUNK, CH, BLK), bf),
            pltpu.VMEM((NCHUNK, CH, BLK), bf),
            pltpu.VMEM((2, ROWS, BLK), bf),
            dma((NCHUNK, 6)), dma((NCHUNK, 6)),
            dma((NCHUNK, 2)), dma((NCHUNK, 2)),
            dma((NCHUNK, 4)), dma((NCHUNK, 4)),
            dma((NPIECE,)), dma((NPIECE,)),
            dma((n_col,)), dma((n_col,)),
            dma((3,)),
        ],
        compiler_params=pltpu.CompilerParams(collective_id=0, has_side_effects=True),
        name="move",
    )(panel_owner, a, ac, b, bc)
    out = pl.pallas_call(
        functools.partial(compute_kernel, n_row),
        out_shape=jax.ShapeDtypeStruct((KB, NCS, BLK, BLK), bf),
        in_specs=[smem, smem, smem, smem, smem, smem, vmem, any_, any_],
        out_specs=vmem,
        scratch_shapes=[
            pltpu.SMEM((2 * KB * CB,), jnp.int32),
            pltpu.VMEM((2 * KB * NZB + 1, BLK, BLK), bf),
            pltpu.VMEM((BLK, 2 * NZA * BLK), bf),
            pltpu.VMEM((2 * NZA * BLK, NCS * BLK), bf),
            dma((2,)),
        ],
        name="product",
    )(panel_owner, atom_size, acg, bc, bcn, cc, panels.reshape(2, KB * NZA, BLK, BLK), b, bn)
    return out.reshape(1, 1, KB, NCS, BLK, BLK)


def solution(mesh):
    placed = (
        P("row", "col", None, None, None, None, None),
        P("row", "col", None, None, None),
        P("row", "col", None, None, None, None),
        P("row", "col", None, None),
        P("row", "col", None, None),
        P(),
        P(),
    )
    return jax.shard_map(
        functools.partial(local, mesh.shape["row"], mesh.shape["col"]),
        mesh=mesh,
        in_specs=placed,
        out_specs=P("row", "col", None, None, None, None),
        check_vma=False,
    )
```

```python
import functools

import jax
import jax.numpy as jnp
from jax import lax
from jax.experimental import pallas as pl
from jax.experimental.pallas import tpu as pltpu
from jax.sharding import PartitionSpec as P

MESH = pl.DeviceIdType.MESH
BLK = 128
KB = 6
NZA = 5
NZB = 8
NCS = 6
CB = 12
NY = 4
NZ = 4
ROWS = KB * NZA * BLK
SLICE = ROWS // NY
NH = 4
NB = KB * NZB
PER = 2
CH = SLICE // PER
HF = CH // 2
NCHUNK = 2 * PER
STRIP = 240
PIECE = 1
RB = 12
NRG = 12
B_FIRST = 4
LEGS = 3


def remote(src, dst, send_sem, recv_sem, device):
    return pltpu.make_async_remote_copy(
        src_ref=src, dst_ref=dst, send_sem=send_sem, recv_sem=recv_sem,
        device_id=device, device_id_type=MESH)


def fox_kernel(n_row, n_col, owner_ref, size_ref, bcs_ref, cc_ref, a_ref, ac_ref, b_ref, bc_ref,
               o_ref, acg_ref, bcn_ref,
               a_buf, sel, r_up, r_dn, l_up, l_dn, t_buf, u_in, d_in, u_out, d_out, full0, full1, hold,
               b_own, b_next, part, lhs, rhs, acs, bns,
               s_y1, v_y1, s_z, v_z, s_y2, v_y2, s_b, v_b, s_r, v_r, s_i, v_i, loc):
    full = (full0, full1)
    me_r = lax.axis_index("row")
    me_c = lax.axis_index("col")
    y = lax.rem(me_c, NY)
    q = me_c // NY
    core = lax.rem(me_r, 2)
    chip = me_r // 2
    zh = lax.rem(chip, NH)
    x = chip // NH
    n_x = n_row // (2 * NH)
    y_p = lax.rem(y + 1, NY)
    y_m = lax.rem(y + NY - 1, NY)
    y_o = lax.rem(y + 2, NY)
    dev_p = (me_r, q * NY + y_p)
    dev_m = (me_r, q * NY + y_m)
    dev_u = (me_r, lax.rem(me_c + NY, n_col))
    dev_d = (me_r, lax.rem(me_c + n_col - NY, n_col))
    to_b = (lax.rem(me_r + n_row - 1, n_row), me_c)
    from_b = (lax.rem(me_r + 1, n_row), me_c)

    def odd_at(px, pz):
        return ((px * NH + pz) * 2 + 1, me_c)

    z_next = lax.rem(zh + 1, NH)
    z_last = lax.rem(zh + NH - 1, NH)
    hop = odd_at(x, z_next)
    hop_back = odd_at(x, z_last)
    last = odd_at(lax.rem(x + n_x - (zh == NH - 2).astype(jnp.int32), n_x), z_next)
    last_back = odd_at(lax.rem(x + (zh == NH - 1).astype(jnp.int32), n_x), z_last)

    barrier = pltpu.get_barrier_semaphore()
    for d in range(1, n_col):
        pl.semaphore_signal(barrier, inc=1, device_id=(me_r, lax.rem(me_c + d, n_col)), device_id_type=MESH)
    pl.semaphore_signal(barrier, inc=1, device_id=to_b, device_id_type=MESH)
    pl.semaphore_signal(barrier, inc=1, device_id=from_b, device_id_type=MESH)

    @pl.when(core == 1)
    def _():
        for dev in (hop, hop_back, last, last_back):
            pl.semaphore_signal(barrier, inc=1, device_id=dev, device_id_type=MESH)

    b_load = pltpu.make_async_copy(b_ref, b_own.at[pl.ds(0, NB)], loc.at[1])
    a_loads = []
    for s in range(2):
        cp = pltpu.make_async_copy(a_ref.at[s], a_buf.at[s], loc.at[3 + s])
        cp.start()
        a_loads.append(cp)
    b_load.start()
    for cp in a_loads:
        cp.wait()
    for s in range(2):
        place = owner_ref[me_r, lax.rem(me_r + s, n_row)]
        f0 = (place == 2 * me_c).astype(jnp.float32).astype(jnp.bfloat16)
        f1 = (place == 2 * me_c + 1).astype(jnp.float32).astype(jnp.bfloat16)

        @pl.loop(0, ROWS // STRIP)
        def _(g):
            at = pl.ds(pl.multiple_of(g * STRIP, STRIP), STRIP)
            sel[s, at, :] = a_buf[0, at, :] * f0 + a_buf[1, at, :] * f1

    pl.semaphore_wait(barrier, n_col + 1 + 4 * core)

    straight = [remote(b_ref.at[pl.ds(k * PIECE, PIECE)], b_next.at[pl.ds(k * PIECE, PIECE)],
                       s_b.at[k], v_b.at[k], to_b) for k in range(NB // PIECE)]
    n_even = (NB - RB) // PIECE
    RG = RB // NRG

    def round_copies(g):
        at = pl.ds(NB - RB + g * RG, RG)
        return (
            remote(b_ref.at[at], hold.at[0, g], s_r.at[g, 0], v_r.at[g, 0], from_b),
            remote(hold.at[0, g], hold.at[1, g], s_r.at[g, 1], v_r.at[g, 1], hop),
            remote(hold.at[1, g], hold.at[2, g], s_r.at[g, 2], v_r.at[g, 2], hop),
            remote(hold.at[2, g], b_next.at[at], s_r.at[g, 3], v_r.at[g, 3], last),
        )

    rounds = [round_copies(g) for g in range(NRG)]
    done = [0, 0]
    legs = [(0, g, k) for k in range(3) for g in range(len(rounds))]

    def more_b(count):
        lo, hi = done[0], min(n_even, done[0] + count)
        done[0] = hi

        @pl.when(core == 0)
        def _():
            for k in range(lo, hi):
                straight[k].start()

    def leg(count):
        lo, hi = done[1], min(len(legs), done[1] + count)
        done[1] = hi

        @pl.when(core == 1)
        def _():
            for _t, g, k in legs[lo:hi]:
                rounds[g][k].wait_recv()
                rounds[g][k + 1].start()

    own_ac = pltpu.make_async_copy(ac_ref, acg_ref.at[me_c], loc.at[0])
    own_ac.start()

    @pl.when(core == 0)
    def _():
        for cps in rounds:
            cps[0].start()

    @pl.when(core == 1)
    def _():
        for cp in straight:
            cp.start()

    idx = []
    for d in range(1, n_col):
        cp = remote(ac_ref, acg_ref.at[me_c], s_i.at[d], v_i.at[d], (me_r, lax.rem(me_c + d, n_col)))
        cp.start()
        idx.append(cp)
    cp = remote(bc_ref, bcn_ref, s_i.at[0], v_i.at[0], to_b)
    cp.start()
    idx.append(cp)

    def rows_of(slice_id, c, off, size):
        return pl.ds(pl.multiple_of(slice_id * SLICE + (c % PER) * CH + off, 16), size)

    def y1(c):
        s = c // PER
        return (
            remote(sel.at[s, rows_of(y_o, c, 0, HF)], l_up.at[c], s_y1.at[c, 0], v_y1.at[c, 0], dev_p),
            remote(sel.at[s, rows_of(y_o, c, HF, HF)], l_dn.at[c], s_y1.at[c, 1], v_y1.at[c, 1], dev_m),
            remote(sel.at[s, rows_of(y_p, c, 0, CH)], r_up.at[c], s_y1.at[c, 2], v_y1.at[c, 2], dev_p),
            remote(sel.at[s, rows_of(y_m, c, 0, CH)], r_dn.at[c], s_y1.at[c, 3], v_y1.at[c, 3], dev_m),
        )

    def zs(c):
        return (
            remote(u_out.at[c], u_in.at[c], s_z.at[c, 0], v_z.at[c, 0], dev_u),
            remote(d_out.at[c], d_in.at[c], s_z.at[c, 1], v_z.at[c, 1], dev_d),
        )

    def y2(c):
        s = c // PER
        own = rows_of(y, c, 0, CH)
        lo = rows_of(y_m, c, 0, HF)
        hi = rows_of(y_p, c, HF, HF)
        return (
            remote(full[s].at[own], full[s].at[own], s_y2.at[c, 0], v_y2.at[c, 0], dev_p),
            remote(full[s].at[own], full[s].at[own], s_y2.at[c, 1], v_y2.at[c, 1], dev_m),
            remote(full[s].at[lo], full[s].at[lo], s_y2.at[c, 2], v_y2.at[c, 2], dev_p),
            remote(full[s].at[hi], full[s].at[hi], s_y2.at[c, 3], v_y2.at[c, 3], dev_m),
        )

    y1s = [y1(c) for c in range(NCHUNK)]
    zss = [zs(c) for c in range(NCHUNK)]
    y2s = [y2(c) for c in range(NCHUNK)]

    def first(c):
        y1s[c][0].start()
        y1s[c][1].start()

    def relay(c):
        s = c // PER
        y1s[c][0].wait_recv()
        at = rows_of(y_p, c, 0, HF)
        sel[s, at, :] = sel[s, at, :] + l_up[c]
        y1s[c][1].wait_recv()
        at = rows_of(y_m, c, HF, HF)
        sel[s, at, :] = sel[s, at, :] + l_dn[c]
        y1s[c][2].start()
        y1s[c][3].start()

    def up(c):
        zss[c][0].wait_recv()
        u_out[c] = t_buf[c] + u_in[c]
        zss[c][0].start()

    def down(c):
        zss[c][1].wait_recv()
        d_out[c] = t_buf[c] + d_in[c]
        zss[c][1].start()

    def gather_slice(c):
        for j in (2, 3):
            y1s[c][j].wait_recv()
        t = sel[c // PER, rows_of(y, c, 0, CH), :] + r_up[c] + r_dn[c]
        t_buf[c] = t

        @pl.when(q == 0)
        def _():
            u_out[c] = t
            zss[c][0].start()

        @pl.when(q == NZ - 1)
        def _():
            d_out[c] = t
            zss[c][1].start()

    def spread(c, value):
        full[c // PER][rows_of(y, c, 0, CH), :] = value
        y2s[c][0].start()
        y2s[c][1].start()

    def chain_a(c):
        @pl.when(q == 1)
        def _():
            up(c)

        @pl.when(q == 2)
        def _():
            down(c)

    def chain_b(c):
        @pl.when(q == 2)
        def _():
            up(c)
            spread(c, u_out[c] + d_in[c])

        @pl.when(q == 1)
        def _():
            down(c)
            spread(c, u_out[c] + d_in[c])

    def chain_c(c):
        @pl.when(q == 0)
        def _():
            zss[c][1].wait_recv()
            spread(c, t_buf[c] + d_in[c])

        @pl.when(q == NZ - 1)
        def _():
            zss[c][0].wait_recv()
            spread(c, t_buf[c] + u_in[c])

    def pass_on(c):
        y2s[c][0].wait_recv()
        y2s[c][2].start()
        y2s[c][1].wait_recv()
        y2s[c][3].start()

    lane = lax.broadcasted_iota(jnp.int32, (BLK, BLK), 1)
    line = lax.broadcasted_iota(jnp.int32, (BLK, BLK), 0)
    b_own[NB] = jnp.zeros((BLK, BLK), jnp.bfloat16)
    b_next[NB] = jnp.zeros((BLK, BLK), jnp.bfloat16)

    def multiply(s, lo, hi):
        k_panel = lax.rem(me_r + s, n_row)
        place = owner_ref[me_r, k_panel]
        holder = place // 2
        slot = lax.rem(place, 2)
        blocks = (b_own, b_next)[s]
        cols = (bcs_ref, bns)[s]

        @pl.loop(lo, hi)
        def _(i):
            targets = [cc_ref[i, 0, t] for t in range(NCS)]
            for m in range(NZA):
                j = acs[holder, m, slot, i]
                width = size_ref[k_panel * KB + j]
                block = full[s][pl.ds(pl.multiple_of((i * NZA + m) * BLK, BLK), BLK), :]
                lhs[:, m * BLK:(m + 1) * BLK] = jnp.where(lane < width, block, jnp.zeros((), jnp.bfloat16))
                found = [cols[j, 0, n] for n in range(NZB)]
                for t in range(NCS):
                    where = jnp.int32(NB)
                    for n in range(NZB):
                        where = jnp.where(found[n] == targets[t], j * NZB + n, where)
                    rhs[m * BLK:(m + 1) * BLK, t * BLK:(t + 1) * BLK] = blocks[where]
            acc = jnp.dot(lhs[...], rhs[...], preferred_element_type=jnp.float32)
            if s == 0:
                part[i] = acc
            else:
                acc = acc + part[i]
                height = size_ref[me_r * KB + i]
                for t in range(NCS):
                    wide = size_ref[me_c * CB + targets[t]]
                    inside = (line < height) & (lane < wide)
                    o_ref[i, t] = jnp.where(inside, acc[:, t * BLK:(t + 1) * BLK], 0.0).astype(jnp.bfloat16)

    def indices():
        own_ac.wait()
        for cp in idx:
            cp.wait()
        pair = [pltpu.make_async_copy(acg_ref, acs, loc.at[2]), pltpu.make_async_copy(bcn_ref, bns, loc.at[0])]
        for cp in pair:
            cp.start()
        for cp in pair:
            cp.wait()
        b_load.wait()

    def landed(s):
        for c in range(s * PER, (s + 1) * PER):
            y2s[c][2].wait_recv()
            y2s[c][3].wait_recv()

    first(0)
    first(1)
    steps = NCHUNK + 5
    more_b(B_FIRST)
    leg(LEGS)
    per = -(-(n_even - B_FIRST) // (steps - 1))
    for c in range(steps):
        for lag, act in ((5, pass_on), (4, chain_c), (3, chain_b), (2, chain_a), (1, gather_slice), (0, relay)):
            if 0 <= c - lag < NCHUNK:
                act(c - lag)
        if c + 2 < NCHUNK:
            first(c + 2)
        more_b(per)
        leg(LEGS)
        if c == steps - 6:
            indices()
    more_b(NB)
    landed(0)
    leg(LEGS * 2)
    multiply(0, 0, KB)
    leg(len(legs))
    landed(1)
    for c in range(NCHUNK):
        for cp in y1s[c]:
            cp.wait_send()
        for cp in y2s[c]:
            cp.wait_send()

        @pl.when(q < NZ - 1)
        def _():
            zss[c][0].wait_send()

        @pl.when(q > 0)
        def _():
            zss[c][1].wait_send()

    @pl.when(core == 0)
    def _():
        for cp in straight[:n_even]:
            cp.wait_send()
        for cps in rounds:
            cps[0].wait_send()
        for cp in straight:
            cp.wait_recv()

    @pl.when(core == 1)
    def _():
        for cp in straight[:n_even]:
            cp.wait_recv()
        for cps in rounds:
            cps[3].wait_recv()
            for cp in cps[1:]:
                cp.wait_send()
        for cp in straight:
            cp.wait_send()

    multiply(1, 0, KB)


def local(n_row, n_col, a_vals, a_cols, b_vals, b_cols, c_cols, panel_owner, atom_size):
    a = a_vals.reshape(2, ROWS, BLK)
    ac = jnp.transpose(a_cols[0, 0], (2, 0, 1))
    b = b_vals.reshape(KB * NZB, BLK, BLK)
    bc = b_cols.reshape(KB, 1, NZB)
    cc = c_cols.reshape(KB, 1, NCS)
    any_ = pl.BlockSpec(memory_space=pl.ANY)
    vmem = pl.BlockSpec(memory_space=pltpu.VMEM)
    smem = pl.BlockSpec(memory_space=pltpu.SMEM)
    bf = jnp.bfloat16
    dma = pltpu.SemaphoreType.DMA
    out, _, _ = pl.pallas_call(
        functools.partial(fox_kernel, n_row, n_col),
        out_shape=(
            jax.ShapeDtypeStruct((KB, NCS, BLK, BLK), bf),
            jax.ShapeDtypeStruct((n_col, NZA, 2, KB), jnp.int32),
            jax.ShapeDtypeStruct((KB, 1, NZB), jnp.int32),
        ),
        in_specs=[smem, smem, smem, smem, any_, any_, any_, any_],
        out_specs=(vmem, any_, any_),
        scratch_shapes=[
            pltpu.VMEM((2, ROWS, BLK), bf),
            pltpu.VMEM((2, ROWS, BLK), bf),
            pltpu.VMEM((NCHUNK, CH, BLK), bf),
            pltpu.VMEM((NCHUNK, CH, BLK), bf),
            pltpu.VMEM((NCHUNK, HF, BLK), bf),
            pltpu.VMEM((NCHUNK, HF, BLK), bf),
            pltpu.VMEM((NCHUNK, CH, BLK), bf),
            pltpu.VMEM((NCHUNK, CH, BLK), bf),
            pltpu.VMEM((NCHUNK, CH, BLK), bf),
            pltpu.VMEM((NCHUNK, CH, BLK), bf),
            pltpu.VMEM((NCHUNK, CH, BLK), bf),
            pltpu.VMEM((ROWS, BLK), bf),
            pltpu.VMEM((ROWS, BLK), bf),
            pltpu.VMEM((3, NRG, RB // NRG, BLK, BLK), bf),
            pltpu.VMEM((NB + 1, BLK, BLK), bf),
            pltpu.VMEM((NB + 1, BLK, BLK), bf),
            pltpu.VMEM((KB, BLK, NCS * BLK), jnp.float32),
            pltpu.VMEM((BLK, NZA * BLK), bf),
            pltpu.VMEM((NZA * BLK, NCS * BLK), bf),
            pltpu.SMEM((n_col, NZA, 2, KB), jnp.int32),
            pltpu.SMEM((KB, 1, NZB), jnp.int32),
            dma((NCHUNK, 4)), dma((NCHUNK, 4)),
            dma((NCHUNK, 2)), dma((NCHUNK, 2)),
            dma((NCHUNK, 4)), dma((NCHUNK, 4)),
            dma((NB // PIECE,)), dma((NB // PIECE,)),
            dma((NRG, 4)), dma((NRG, 4)),
            dma((n_col,)), dma((n_col,)),
            dma((5,)),
        ],
        compiler_params=pltpu.CompilerParams(collective_id=0, has_side_effects=True),
        name="fox",
    )(panel_owner, atom_size, bc, cc, a, ac, b, bc)
    return out.reshape(1, 1, KB, NCS, BLK, BLK)


def solution(mesh):
    placed = (
        P("row", "col", None, None, None, None, None),
        P("row", "col", None, None, None),
        P("row", "col", None, None, None, None),
        P("row", "col", None, None),
        P("row", "col", None, None),
        P(),
        P(),
    )
    return jax.shard_map(
        functools.partial(local, mesh.shape["row"], mesh.shape["col"]),
        mesh=mesh,
        in_specs=placed,
        out_specs=P("row", "col", None, None, None, None),
        check_vma=False,
    )
```

```python
import functools

import jax
import jax.numpy as jnp
from jax import lax
from jax.experimental import pallas as pl
from jax.experimental.pallas import tpu as pltpu
from jax.sharding import PartitionSpec as P

MESH = pl.DeviceIdType.MESH
BLK = 128
KB = 6
NZA = 5
NZB = 8
NCS = 6
CB = 12
NY = 4
NZ = 4
ROWS = KB * NZA * BLK
SLICE = ROWS // NY
NH = 4
NB = KB * NZB
PER = 2
CH = SLICE // PER
HF = CH // 2
NCHUNK = 2 * PER
STRIP = 240
RB = 8
NPB = 2 * NZB
FRONT = 8
MID = 3
L_FRONT = 8
L_MID = 2
L_LATE = 8


def remote(src, dst, send_sem, recv_sem, device):
    return pltpu.make_async_remote_copy(
        src_ref=src, dst_ref=dst, send_sem=send_sem, recv_sem=recv_sem,
        device_id=device, device_id_type=MESH)


def fox_kernel(n_row, n_col, owner_ref, size_ref, bcs_ref, cc_ref, a_ref, ac_ref, b_ref, bc_ref,
               o_ref, acg_ref, bcn_ref,
               a_buf, sel, r_up, r_dn, l_up, l_dn, t_buf, u_in, d_in, u_out, d_out, full0, full1, hold,
               b_own, b_n0, b_n1, b_n2, part, lhs, rhs, lhs2, rhs2, acs, bns,
               s_y1, v_y1, s_z, v_z, s_y2, v_y2, s_b, v_b, s_r, v_r, s_i, v_i, loc):
    full = (full0, full1)
    b_next = (b_n0, b_n1, b_n2)
    me_r = lax.axis_index("row")
    me_c = lax.axis_index("col")
    y = lax.rem(me_c, NY)
    q = me_c // NY
    core = lax.rem(me_r, 2)
    chip = me_r // 2
    zh = lax.rem(chip, NH)
    x = chip // NH
    n_x = n_row // (2 * NH)
    y_p = lax.rem(y + 1, NY)
    y_m = lax.rem(y + NY - 1, NY)
    y_o = lax.rem(y + 2, NY)
    dev_p = (me_r, q * NY + y_p)
    dev_m = (me_r, q * NY + y_m)
    dev_u = (me_r, lax.rem(me_c + NY, n_col))
    dev_d = (me_r, lax.rem(me_c + n_col - NY, n_col))
    to_b = (lax.rem(me_r + n_row - 1, n_row), me_c)
    from_b = (lax.rem(me_r + 1, n_row), me_c)

    def odd_at(px, pz):
        return ((px * NH + pz) * 2 + 1, me_c)

    z_next = lax.rem(zh + 1, NH)
    z_last = lax.rem(zh + NH - 1, NH)
    hop = odd_at(x, z_next)
    hop_back = odd_at(x, z_last)
    last = odd_at(lax.rem(x + n_x - (zh == NH - 2).astype(jnp.int32), n_x), z_next)
    last_back = odd_at(lax.rem(x + (zh == NH - 1).astype(jnp.int32), n_x), z_last)

    barrier = pltpu.get_barrier_semaphore()
    for d in range(1, n_col):
        pl.semaphore_signal(barrier, inc=1, device_id=(me_r, lax.rem(me_c + d, n_col)), device_id_type=MESH)
    pl.semaphore_signal(barrier, inc=1, device_id=to_b, device_id_type=MESH)
    pl.semaphore_signal(barrier, inc=1, device_id=from_b, device_id_type=MESH)

    @pl.when(core == 1)
    def _():
        for dev in (hop, hop_back, last, last_back):
            pl.semaphore_signal(barrier, inc=1, device_id=dev, device_id_type=MESH)

    b_load = pltpu.make_async_copy(b_ref, b_own.at[pl.ds(0, NB)], loc.at[1])
    a_loads = []
    for s in range(2):
        cp = pltpu.make_async_copy(a_ref.at[s], a_buf.at[s], loc.at[3 + s])
        cp.start()
        a_loads.append(cp)
    b_load.start()
    for cp in a_loads:
        cp.wait()
    for s in range(2):
        place = owner_ref[me_r, lax.rem(me_r + s, n_row)]
        f0 = (place == 2 * me_c).astype(jnp.float32).astype(jnp.bfloat16)
        f1 = (place == 2 * me_c + 1).astype(jnp.float32).astype(jnp.bfloat16)

        @pl.loop(0, ROWS // STRIP)
        def _(g):
            at = pl.ds(pl.multiple_of(g * STRIP, STRIP), STRIP)
            sel[s, at, :] = a_buf[0, at, :] * f0 + a_buf[1, at, :] * f1

    pl.semaphore_wait(barrier, n_col + 1 + 4 * core)

    straight = [remote(b_ref.at[k], b_next[k // NPB].at[k % NPB],
                       s_b.at[k], v_b.at[k], to_b) for k in range(NB)]
    n_even = NB - RB

    def round_copies(g):
        k = NB - RB + g
        return (
            remote(b_ref.at[k], hold.at[0, g], s_r.at[g, 0], v_r.at[g, 0], from_b),
            remote(hold.at[0, g], hold.at[1, g], s_r.at[g, 1], v_r.at[g, 1], hop),
            remote(hold.at[1, g], hold.at[2, g], s_r.at[g, 2], v_r.at[g, 2], hop),
            remote(hold.at[2, g], b_next[k // NPB].at[k % NPB], s_r.at[g, 3], v_r.at[g, 3], last),
        )

    rounds = [round_copies(g) for g in range(RB)]
    done = [0, 0]
    legs = [(0, g, k) for k in range(3) for g in range(len(rounds))]

    def more_b(count):
        lo, hi = done[0], min(n_even, done[0] + count)
        done[0] = hi

        @pl.when(core == 0)
        def _():
            for k in range(lo, hi):
                straight[k].start()

    def leg(count):
        lo, hi = done[1], min(len(legs), done[1] + count)
        done[1] = hi

        @pl.when(core == 1)
        def _():
            for _t, g, k in legs[lo:hi]:
                rounds[g][k].wait_recv()
                rounds[g][k + 1].start()

    own_ac = pltpu.make_async_copy(ac_ref, acg_ref.at[me_c], loc.at[0])
    own_ac.start()

    @pl.when(core == 0)
    def _():
        for cps in rounds:
            cps[0].start()

    @pl.when(core == 1)
    def _():
        for cp in straight:
            cp.start()

    idx = []
    for d in range(1, n_col):
        cp = remote(ac_ref, acg_ref.at[me_c], s_i.at[d], v_i.at[d], (me_r, lax.rem(me_c + d, n_col)))
        cp.start()
        idx.append(cp)
    cp = remote(bc_ref, bcn_ref, s_i.at[0], v_i.at[0], to_b)
    cp.start()
    idx.append(cp)

    def rows_of(slice_id, c, off, size):
        return pl.ds(pl.multiple_of(slice_id * SLICE + (c % PER) * CH + off, 16), size)

    def y1(c):
        s = c // PER
        return (
            remote(sel.at[s, rows_of(y_o, c, 0, HF)], l_up.at[c], s_y1.at[c, 0], v_y1.at[c, 0], dev_p),
            remote(sel.at[s, rows_of(y_o, c, HF, HF)], l_dn.at[c], s_y1.at[c, 1], v_y1.at[c, 1], dev_m),
            remote(sel.at[s, rows_of(y_p, c, 0, CH)], r_up.at[c], s_y1.at[c, 2], v_y1.at[c, 2], dev_p),
            remote(sel.at[s, rows_of(y_m, c, 0, CH)], r_dn.at[c], s_y1.at[c, 3], v_y1.at[c, 3], dev_m),
        )

    def zs(c):
        return (
            remote(u_out.at[c], u_in.at[c], s_z.at[c, 0], v_z.at[c, 0], dev_u),
            remote(d_out.at[c], d_in.at[c], s_z.at[c, 1], v_z.at[c, 1], dev_d),
        )

    def y2(c):
        s = c // PER
        own = rows_of(y, c, 0, CH)
        lo = rows_of(y_m, c, 0, HF)
        hi = rows_of(y_p, c, HF, HF)
        return (
            remote(full[s].at[own], full[s].at[own], s_y2.at[c, 0], v_y2.at[c, 0], dev_p),
            remote(full[s].at[own], full[s].at[own], s_y2.at[c, 1], v_y2.at[c, 1], dev_m),
            remote(full[s].at[lo], full[s].at[lo], s_y2.at[c, 2], v_y2.at[c, 2], dev_p),
            remote(full[s].at[hi], full[s].at[hi], s_y2.at[c, 3], v_y2.at[c, 3], dev_m),
        )

    y1s = [y1(c) for c in range(NCHUNK)]
    zss = [zs(c) for c in range(NCHUNK)]
    y2s = [y2(c) for c in range(NCHUNK)]

    def first(c):
        y1s[c][0].start()
        y1s[c][1].start()

    def relay(c):
        s = c // PER
        y1s[c][0].wait_recv()
        at = rows_of(y_p, c, 0, HF)
        sel[s, at, :] = sel[s, at, :] + l_up[c]
        y1s[c][1].wait_recv()
        at = rows_of(y_m, c, HF, HF)
        sel[s, at, :] = sel[s, at, :] + l_dn[c]
        y1s[c][2].start()
        y1s[c][3].start()

    def up(c):
        zss[c][0].wait_recv()
        u_out[c] = t_buf[c] + u_in[c]
        zss[c][0].start()

    def down(c):
        zss[c][1].wait_recv()
        d_out[c] = t_buf[c] + d_in[c]
        zss[c][1].start()

    def gather_slice(c):
        for j in (2, 3):
            y1s[c][j].wait_recv()
        t = sel[c // PER, rows_of(y, c, 0, CH), :] + r_up[c] + r_dn[c]
        t_buf[c] = t

        @pl.when(q == 0)
        def _():
            u_out[c] = t
            zss[c][0].start()

        @pl.when(q == NZ - 1)
        def _():
            d_out[c] = t
            zss[c][1].start()

    def spread(c, value):
        full[c // PER][rows_of(y, c, 0, CH), :] = value
        y2s[c][0].start()
        y2s[c][1].start()

    def chain_a(c):
        @pl.when(q == 1)
        def _():
            up(c)

        @pl.when(q == 2)
        def _():
            down(c)

    def chain_b(c):
        @pl.when(q == 2)
        def _():
            up(c)
            spread(c, u_out[c] + d_in[c])

        @pl.when(q == 1)
        def _():
            down(c)
            spread(c, u_out[c] + d_in[c])

    def chain_c(c):
        @pl.when(q == 0)
        def _():
            zss[c][1].wait_recv()
            spread(c, t_buf[c] + d_in[c])

        @pl.when(q == NZ - 1)
        def _():
            zss[c][0].wait_recv()
            spread(c, t_buf[c] + u_in[c])

    def pass_on(c):
        y2s[c][0].wait_recv()
        y2s[c][2].start()
        y2s[c][1].wait_recv()
        y2s[c][3].start()

    lane = lax.broadcasted_iota(jnp.int32, (BLK, BLK), 1)
    line = lax.broadcasted_iota(jnp.int32, (BLK, BLK), 0)
    b_own[NB] = jnp.zeros((BLK, BLK), jnp.bfloat16)
    for ref in b_next:
        ref[NPB] = jnp.zeros((BLK, BLK), jnp.bfloat16)

    def multiply_first():
        place = owner_ref[me_r, me_r]
        holder = place // 2
        slot = lax.rem(place, 2)

        @pl.loop(0, KB)
        def _(i):
            targets = [cc_ref[i, 0, t] for t in range(NCS)]
            for m in range(NZA):
                j = acs[holder, m, slot, i]
                width = size_ref[me_r * KB + j]
                block = full0[pl.ds(pl.multiple_of((i * NZA + m) * BLK, BLK), BLK), :]
                lhs[:, m * BLK:(m + 1) * BLK] = jnp.where(lane < width, block, jnp.zeros((), jnp.bfloat16))
                found = [bcs_ref[j, 0, n] for n in range(NZB)]
                for t in range(NCS):
                    where = jnp.int32(NB)
                    for n in range(NZB):
                        where = jnp.where(found[n] == targets[t], j * NZB + n, where)
                    rhs[m * BLK:(m + 1) * BLK, t * BLK:(t + 1) * BLK] = b_own[where]
            part[i] = jnp.dot(lhs[...], rhs[...], preferred_element_type=jnp.float32)

    def multiply_pair(p):
        k_panel = lax.rem(me_r + 1, n_row)
        place = owner_ref[me_r, k_panel]
        holder = place // 2
        slot = lax.rem(place, 2)

        @pl.loop(0, KB)
        def _(i):
            targets = [cc_ref[i, 0, t] for t in range(NCS)]
            stored = [acs[holder, m, slot, i] for m in range(NZA)]
            for e in range(2):
                j = 2 * p + e
                width = size_ref[k_panel * KB + j]
                block = None
                for m in range(NZA):
                    flag = (stored[m] == j).astype(jnp.float32).astype(jnp.bfloat16)
                    one = full1[pl.ds(pl.multiple_of((i * NZA + m) * BLK, BLK), BLK), :] * flag
                    block = one if block is None else block + one
                lhs2[:, e * BLK:(e + 1) * BLK] = jnp.where(lane < width, block, jnp.zeros((), jnp.bfloat16))
                found = [bns[j, 0, n] for n in range(NZB)]
                for t in range(NCS):
                    where = jnp.int32(NPB)
                    for n in range(NZB):
                        where = jnp.where(found[n] == targets[t], e * NZB + n, where)
                    rhs2[e * BLK:(e + 1) * BLK, t * BLK:(t + 1) * BLK] = b_next[p][where]
            acc = part[i] + jnp.dot(lhs2[...], rhs2[...], preferred_element_type=jnp.float32)
            if p < 2:
                part[i] = acc
            else:
                height = size_ref[me_r * KB + i]
                for t in range(NCS):
                    wide = size_ref[me_c * CB + targets[t]]
                    inside = (line < height) & (lane < wide)
                    o_ref[i, t] = jnp.where(inside, acc[:, t * BLK:(t + 1) * BLK], 0.0).astype(jnp.bfloat16)

    def have_pair(p):
        @pl.when(core == 0)
        def _():
            for k in range(p * NPB, (p + 1) * NPB):
                straight[k].wait_recv()

        @pl.when(core == 1)
        def _():
            for k in range(p * NPB, (p + 1) * NPB):
                if k < n_even:
                    straight[k].wait_recv()
                else:
                    rounds[k - n_even][3].wait_recv()

    def indices():
        own_ac.wait()
        for cp in idx:
            cp.wait()
        pair = [pltpu.make_async_copy(acg_ref, acs, loc.at[2]), pltpu.make_async_copy(bcn_ref, bns, loc.at[0])]
        for cp in pair:
            cp.start()
        for cp in pair:
            cp.wait()
        b_load.wait()

    def landed(s):
        for c in range(s * PER, (s + 1) * PER):
            y2s[c][2].wait_recv()
            y2s[c][3].wait_recv()

    first(0)
    first(1)
    steps = NCHUNK + 5
    more_b(FRONT)
    leg(L_FRONT)
    for c in range(steps):
        for lag, act in ((5, pass_on), (4, chain_c), (3, chain_b), (2, chain_a), (1, gather_slice), (0, relay)):
            if 0 <= c - lag < NCHUNK:
                act(c - lag)
        if c + 2 < NCHUNK:
            first(c + 2)
        more_b(MID if c < NCHUNK + 5 else NB)
        leg(L_MID if c < NCHUNK + 5 else L_LATE)
        if c == steps - 4:
            indices()
    more_b(NB)
    more_b(NB)
    landed(0)
    leg(L_LATE)
    multiply_first()
    leg(len(legs))
    landed(1)
    have_pair(0)
    multiply_pair(0)
    have_pair(1)
    multiply_pair(1)
    for c in range(NCHUNK):
        for cp in y1s[c]:
            cp.wait_send()
        for cp in y2s[c]:
            cp.wait_send()

        @pl.when(q < NZ - 1)
        def _():
            zss[c][0].wait_send()

        @pl.when(q > 0)
        def _():
            zss[c][1].wait_send()

    @pl.when(core == 0)
    def _():
        for cp in straight[:n_even]:
            cp.wait_send()
        for cps in rounds:
            cps[0].wait_send()

    @pl.when(core == 1)
    def _():
        for cps in rounds:
            for cp in cps[1:]:
                cp.wait_send()
        for cp in straight:
            cp.wait_send()

    have_pair(2)
    multiply_pair(2)


def local(n_row, n_col, a_vals, a_cols, b_vals, b_cols, c_cols, panel_owner, atom_size):
    a = a_vals.reshape(2, ROWS, BLK)
    ac = jnp.transpose(a_cols[0, 0], (2, 0, 1))
    b = b_vals.reshape(KB * NZB, BLK, BLK)
    bc = b_cols.reshape(KB, 1, NZB)
    cc = c_cols.reshape(KB, 1, NCS)
    any_ = pl.BlockSpec(memory_space=pl.ANY)
    vmem = pl.BlockSpec(memory_space=pltpu.VMEM)
    smem = pl.BlockSpec(memory_space=pltpu.SMEM)
    bf = jnp.bfloat16
    dma = pltpu.SemaphoreType.DMA
    out, _, _ = pl.pallas_call(
        functools.partial(fox_kernel, n_row, n_col),
        out_shape=(
            jax.ShapeDtypeStruct((KB, NCS, BLK, BLK), bf),
            jax.ShapeDtypeStruct((n_col, NZA, 2, KB), jnp.int32),
            jax.ShapeDtypeStruct((KB, 1, NZB), jnp.int32),
        ),
        in_specs=[smem, smem, smem, smem, any_, any_, any_, any_],
        out_specs=(vmem, any_, any_),
        scratch_shapes=[
            pltpu.VMEM((2, ROWS, BLK), bf),
            pltpu.VMEM((2, ROWS, BLK), bf),
            pltpu.VMEM((NCHUNK, CH, BLK), bf),
            pltpu.VMEM((NCHUNK, CH, BLK), bf),
            pltpu.VMEM((NCHUNK, HF, BLK), bf),
            pltpu.VMEM((NCHUNK, HF, BLK), bf),
            pltpu.VMEM((NCHUNK, CH, BLK), bf),
            pltpu.VMEM((NCHUNK, CH, BLK), bf),
            pltpu.VMEM((NCHUNK, CH, BLK), bf),
            pltpu.VMEM((NCHUNK, CH, BLK), bf),
            pltpu.VMEM((NCHUNK, CH, BLK), bf),
            pltpu.VMEM((ROWS, BLK), bf),
            pltpu.VMEM((ROWS, BLK), bf),
            pltpu.VMEM((3, RB, BLK, BLK), bf),
            pltpu.VMEM((NB + 1, BLK, BLK), bf),
            pltpu.VMEM((NPB + 1, BLK, BLK), bf),
            pltpu.VMEM((NPB + 1, BLK, BLK), bf),
            pltpu.VMEM((NPB + 1, BLK, BLK), bf),
            pltpu.VMEM((KB, BLK, NCS * BLK), jnp.float32),
            pltpu.VMEM((BLK, NZA * BLK), bf),
            pltpu.VMEM((NZA * BLK, NCS * BLK), bf),
            pltpu.VMEM((BLK, 2 * BLK), bf),
            pltpu.VMEM((2 * BLK, NCS * BLK), bf),
            pltpu.SMEM((n_col, NZA, 2, KB), jnp.int32),
            pltpu.SMEM((KB, 1, NZB), jnp.int32),
            dma((NCHUNK, 4)), dma((NCHUNK, 4)),
            dma((NCHUNK, 2)), dma((NCHUNK, 2)),
            dma((NCHUNK, 4)), dma((NCHUNK, 4)),
            dma((NB,)), dma((NB,)),
            dma((RB, 4)), dma((RB, 4)),
            dma((n_col,)), dma((n_col,)),
            dma((5,)),
        ],
        compiler_params=pltpu.CompilerParams(collective_id=0, has_side_effects=True),
        name="fox",
    )(panel_owner, atom_size, bc, cc, a, ac, b, bc)
    return out.reshape(1, 1, KB, NCS, BLK, BLK)


def solution(mesh):
    placed = (
        P("row", "col", None, None, None, None, None),
        P("row", "col", None, None, None),
        P("row", "col", None, None, None, None),
        P("row", "col", None, None),
        P("row", "col", None, None),
        P(),
        P(),
    )
    return jax.shard_map(
        functools.partial(local, mesh.shape["row"], mesh.shape["col"]),
        mesh=mesh,
        in_specs=placed,
        out_specs=P("row", "col", None, None, None, None),
        check_vma=False,
    )
```

```python
import functools

import jax
import jax.numpy as jnp
from jax import lax
from jax.experimental import pallas as pl
from jax.experimental.pallas import tpu as pltpu
from jax.sharding import PartitionSpec as P

MESH = pl.DeviceIdType.MESH
BLK = 128
KB = 6
NZA = 5
NZB = 8
NCS = 6
CB = 12
NY = 4
NZ = 4
ROWS = KB * NZA * BLK
SLICE = ROWS // NY
NH = 4
NB = KB * NZB
PER = 2
CH = SLICE // PER
HF = CH // 2
NCHUNK = 2 * PER
STRIP = 240
RB = 8
NPB = 2 * NZB
FRONT = 8
MID = 3
L_FRONT = 8
L_MID = 2
L_LATE = 8


def remote(src, dst, send_sem, recv_sem, device):
    return pltpu.make_async_remote_copy(
        src_ref=src, dst_ref=dst, send_sem=send_sem, recv_sem=recv_sem,
        device_id=device, device_id_type=MESH)


def fox_kernel(n_row, n_col, owner_ref, size_ref, bcs_ref, cc_ref, a_ref, ac_ref, b_ref, bc_ref,
               o_ref, acg_ref, bcn_ref,
               a_buf, sel, r_up, r_dn, l_up, l_dn, t_buf, u_in, d_in, u_out, d_out, full0, full1, hold,
               b_own, b_n0, b_n1, b_n2, part, lhs, rhs, lhs2, rhs2, acs, bns,
               s_y1, v_y1, s_z, v_z, s_y2, v_y2, s_b, v_b, s_r, v_r, s_i, v_i, loc):
    full = (full0, full1)
    b_next = (b_n0, b_n1, b_n2)
    me_r = lax.axis_index("row")
    me_c = lax.axis_index("col")
    y = lax.rem(me_c, NY)
    q = me_c // NY
    core = lax.rem(me_r, 2)
    chip = me_r // 2
    zh = lax.rem(chip, NH)
    x = chip // NH
    n_x = n_row // (2 * NH)
    y_p = lax.rem(y + 1, NY)
    y_m = lax.rem(y + NY - 1, NY)
    y_o = lax.rem(y + 2, NY)
    dev_p = (me_r, q * NY + y_p)
    dev_m = (me_r, q * NY + y_m)
    dev_u = (me_r, lax.rem(me_c + NY, n_col))
    dev_d = (me_r, lax.rem(me_c + n_col - NY, n_col))
    to_b = (lax.rem(me_r + n_row - 1, n_row), me_c)
    from_b = (lax.rem(me_r + 1, n_row), me_c)

    def odd_at(px, pz):
        return ((px * NH + pz) * 2 + 1, me_c)

    z_next = lax.rem(zh + 1, NH)
    z_last = lax.rem(zh + NH - 1, NH)
    hop = odd_at(x, z_next)
    hop_back = odd_at(x, z_last)
    last = odd_at(lax.rem(x + n_x - (zh == NH - 2).astype(jnp.int32), n_x), z_next)
    last_back = odd_at(lax.rem(x + (zh == NH - 1).astype(jnp.int32), n_x), z_last)

    barrier = pltpu.get_barrier_semaphore()
    for d in range(1, n_col):
        pl.semaphore_signal(barrier, inc=1, device_id=(me_r, lax.rem(me_c + d, n_col)), device_id_type=MESH)
    pl.semaphore_signal(barrier, inc=1, device_id=to_b, device_id_type=MESH)
    pl.semaphore_signal(barrier, inc=1, device_id=from_b, device_id_type=MESH)

    @pl.when(core == 1)
    def _():
        for dev in (hop, hop_back, last, last_back):
            pl.semaphore_signal(barrier, inc=1, device_id=dev, device_id_type=MESH)

    b_load = pltpu.make_async_copy(b_ref, b_own.at[pl.ds(0, NB)], loc.at[1])
    a_loads = []
    for s in range(2):
        cp = pltpu.make_async_copy(a_ref.at[s], a_buf.at[s], loc.at[3 + s])
        cp.start()
        a_loads.append(cp)
    b_load.start()
    for cp in a_loads:
        cp.wait()
    for s in range(2):
        place = owner_ref[me_r, lax.rem(me_r + s, n_row)]
        f0 = (place == 2 * me_c).astype(jnp.float32).astype(jnp.bfloat16)
        f1 = (place == 2 * me_c + 1).astype(jnp.float32).astype(jnp.bfloat16)

        @pl.loop(0, ROWS // STRIP)
        def _(g):
            at = pl.ds(pl.multiple_of(g * STRIP, STRIP), STRIP)
            sel[s, at, :] = a_buf[0, at, :] * f0 + a_buf[1, at, :] * f1

    pl.semaphore_wait(barrier, n_col + 1 + 4 * core)

    straight = [remote(b_ref.at[k], b_next[k // NPB].at[k % NPB],
                       s_b.at[k], v_b.at[k], to_b) for k in range(NB)]
    n_even = NB - RB

    def round_copies(g):
        k = NB - RB + g
        return (
            remote(b_ref.at[k], hold.at[0, g], s_r.at[g, 0], v_r.at[g, 0], from_b),
            remote(hold.at[0, g], hold.at[1, g], s_r.at[g, 1], v_r.at[g, 1], hop),
            remote(hold.at[1, g], hold.at[2, g], s_r.at[g, 2], v_r.at[g, 2], hop),
            remote(hold.at[2, g], b_next[k // NPB].at[k % NPB], s_r.at[g, 3], v_r.at[g, 3], last),
        )

    rounds = [round_copies(g) for g in range(RB)]
    done = [0, 0]
    legs = [(0, g, k) for k in range(3) for g in range(len(rounds))]

    def more_b(count):
        lo, hi = done[0], min(n_even, done[0] + count)
        done[0] = hi

        @pl.when(core == 0)
        def _():
            for k in range(lo, hi):
                straight[k].start()

    def leg(count):
        lo, hi = done[1], min(len(legs), done[1] + count)
        done[1] = hi

        @pl.when(core == 1)
        def _():
            for _t, g, k in legs[lo:hi]:
                rounds[g][k].wait_recv()
                rounds[g][k + 1].start()

    own_ac = pltpu.make_async_copy(ac_ref, acg_ref.at[me_c], loc.at[0])
    own_ac.start()

    @pl.when(core == 0)
    def _():
        for cps in rounds:
            cps[0].start()

    @pl.when(core == 1)
    def _():
        for cp in straight:
            cp.start()

    idx = []
    for d in range(1, n_col):
        cp = remote(ac_ref, acg_ref.at[me_c], s_i.at[d], v_i.at[d], (me_r, lax.rem(me_c + d, n_col)))
        cp.start()
        idx.append(cp)
    cp = remote(bc_ref, bcn_ref, s_i.at[0], v_i.at[0], to_b)
    cp.start()
    idx.append(cp)

    def rows_of(slice_id, c, off, size):
        return pl.ds(pl.multiple_of(slice_id * SLICE + (c % PER) * CH + off, 16), size)

    def y1(c):
        s = c // PER
        return (
            remote(sel.at[s, rows_of(y_o, c, 0, HF)], l_up.at[c], s_y1.at[c, 0], v_y1.at[c, 0], dev_p),
            remote(sel.at[s, rows_of(y_o, c, HF, HF)], l_dn.at[c], s_y1.at[c, 1], v_y1.at[c, 1], dev_m),
            remote(sel.at[s, rows_of(y_p, c, 0, CH)], r_up.at[c], s_y1.at[c, 2], v_y1.at[c, 2], dev_p),
            remote(sel.at[s, rows_of(y_m, c, 0, CH)], r_dn.at[c], s_y1.at[c, 3], v_y1.at[c, 3], dev_m),
        )

    def zs(c):
        return (
            remote(u_out.at[c], u_in.at[c], s_z.at[c, 0], v_z.at[c, 0], dev_u),
            remote(d_out.at[c], d_in.at[c], s_z.at[c, 1], v_z.at[c, 1], dev_d),
        )

    def y2(c):
        s = c // PER
        own = rows_of(y, c, 0, CH)
        lo = rows_of(y_m, c, 0, HF)
        hi = rows_of(y_p, c, HF, HF)
        return (
            remote(full[s].at[own], full[s].at[own], s_y2.at[c, 0], v_y2.at[c, 0], dev_p),
            remote(full[s].at[own], full[s].at[own], s_y2.at[c, 1], v_y2.at[c, 1], dev_m),
            remote(full[s].at[lo], full[s].at[lo], s_y2.at[c, 2], v_y2.at[c, 2], dev_p),
            remote(full[s].at[hi], full[s].at[hi], s_y2.at[c, 3], v_y2.at[c, 3], dev_m),
        )

    y1s = [y1(c) for c in range(NCHUNK)]
    zss = [zs(c) for c in range(NCHUNK)]
    y2s = [y2(c) for c in range(NCHUNK)]

    def first(c):
        y1s[c][0].start()
        y1s[c][1].start()

    def relay(c):
        s = c // PER
        y1s[c][0].wait_recv()
        at = rows_of(y_p, c, 0, HF)
        sel[s, at, :] = sel[s, at, :] + l_up[c]
        y1s[c][1].wait_recv()
        at = rows_of(y_m, c, HF, HF)
        sel[s, at, :] = sel[s, at, :] + l_dn[c]
        y1s[c][2].start()
        y1s[c][3].start()

    def up(c):
        zss[c][0].wait_recv()
        u_out[c] = t_buf[c] + u_in[c]
        zss[c][0].start()

    def down(c):
        zss[c][1].wait_recv()
        d_out[c] = t_buf[c] + d_in[c]
        zss[c][1].start()

    def gather_slice(c):
        for j in (2, 3):
            y1s[c][j].wait_recv()
        t = sel[c // PER, rows_of(y, c, 0, CH), :] + r_up[c] + r_dn[c]
        t_buf[c] = t

        @pl.when(q == 0)
        def _():
            u_out[c] = t
            zss[c][0].start()

        @pl.when(q == NZ - 1)
        def _():
            d_out[c] = t
            zss[c][1].start()

    def spread(c, value):
        full[c // PER][rows_of(y, c, 0, CH), :] = value
        y2s[c][0].start()
        y2s[c][1].start()

    def chain_a(c):
        @pl.when(q == 1)
        def _():
            up(c)

        @pl.when(q == 2)
        def _():
            down(c)

    def chain_b(c):
        @pl.when(q == 2)
        def _():
            up(c)
            spread(c, u_out[c] + d_in[c])

        @pl.when(q == 1)
        def _():
            down(c)
            spread(c, u_out[c] + d_in[c])

    def chain_c(c):
        @pl.when(q == 0)
        def _():
            zss[c][1].wait_recv()
            spread(c, t_buf[c] + d_in[c])

        @pl.when(q == NZ - 1)
        def _():
            zss[c][0].wait_recv()
            spread(c, t_buf[c] + u_in[c])

    def pass_on(c):
        y2s[c][0].wait_recv()
        y2s[c][2].start()
        y2s[c][1].wait_recv()
        y2s[c][3].start()

    lane = lax.broadcasted_iota(jnp.int32, (BLK, BLK), 1)
    line = lax.broadcasted_iota(jnp.int32, (BLK, BLK), 0)
    b_own[NB] = jnp.zeros((BLK, BLK), jnp.bfloat16)
    for ref in b_next:
        ref[NPB] = jnp.zeros((BLK, BLK), jnp.bfloat16)

    def multiply_first():
        place = owner_ref[me_r, me_r]
        holder = place // 2
        slot = lax.rem(place, 2)

        @pl.loop(0, KB)
        def _(i):
            targets = [cc_ref[i, 0, t] for t in range(NCS)]
            for m in range(NZA):
                j = acs[holder, m, slot, i]
                width = size_ref[me_r * KB + j]
                block = full0[pl.ds(pl.multiple_of((i * NZA + m) * BLK, BLK), BLK), :]
                lhs[:, m * BLK:(m + 1) * BLK] = jnp.where(lane < width, block, jnp.zeros((), jnp.bfloat16))
                found = [bcs_ref[j, 0, n] for n in range(NZB)]
                for t in range(NCS):
                    where = jnp.int32(NB)
                    for n in range(NZB):
                        where = jnp.where(found[n] == targets[t], j * NZB + n, where)
                    rhs[m * BLK:(m + 1) * BLK, t * BLK:(t + 1) * BLK] = b_own[where]
            part[i] = jnp.dot(lhs[...], rhs[...], preferred_element_type=jnp.float32)

    def multiply_pair(p):
        k_panel = lax.rem(me_r + 1, n_row)
        place = owner_ref[me_r, k_panel]
        holder = place // 2
        slot = lax.rem(place, 2)

        @pl.loop(0, KB)
        def _(i):
            targets = [cc_ref[i, 0, t] for t in range(NCS)]
            stored = [acs[holder, m, slot, i] for m in range(NZA)]
            for e in range(2):
                j = 2 * p + e
                width = size_ref[k_panel * KB + j]
                block = None
                for m in range(NZA):
                    flag = (stored[m] == j).astype(jnp.float32).astype(jnp.bfloat16)
                    one = full1[pl.ds(pl.multiple_of((i * NZA + m) * BLK, BLK), BLK), :] * flag
                    block = one if block is None else block + one
                lhs2[:, e * BLK:(e + 1) * BLK] = jnp.where(lane < width, block, jnp.zeros((), jnp.bfloat16))
                found = [bns[j, 0, n] for n in range(NZB)]
                for t in range(NCS):
                    where = jnp.int32(NPB)
                    for n in range(NZB):
                        where = jnp.where(found[n] == targets[t], e * NZB + n, where)
                    rhs2[e * BLK:(e + 1) * BLK, t * BLK:(t + 1) * BLK] = b_next[p][where]
            acc = part[i] + jnp.dot(lhs2[...], rhs2[...], preferred_element_type=jnp.float32)
            if p < 2:
                part[i] = acc
            else:
                height = size_ref[me_r * KB + i]
                for t in range(NCS):
                    wide = size_ref[me_c * CB + targets[t]]
                    inside = (line < height) & (lane < wide)
                    o_ref[i, t] = jnp.where(inside, acc[:, t * BLK:(t + 1) * BLK], 0.0).astype(jnp.bfloat16)

    def have_pair(p):
        @pl.when(core == 0)
        def _():
            for k in range(p * NPB, (p + 1) * NPB):
                straight[k].wait_recv()

        @pl.when(core == 1)
        def _():
            for k in range(p * NPB, (p + 1) * NPB):
                if k < n_even:
                    straight[k].wait_recv()
                else:
                    rounds[k - n_even][3].wait_recv()

    def indices():
        own_ac.wait()
        for cp in idx:
            cp.wait()
        pair = [pltpu.make_async_copy(acg_ref, acs, loc.at[2]), pltpu.make_async_copy(bcn_ref, bns, loc.at[0])]
        for cp in pair:
            cp.start()
        for cp in pair:
            cp.wait()
        b_load.wait()

    def landed(s):
        for c in range(s * PER, (s + 1) * PER):
            y2s[c][2].wait_recv()
            y2s[c][3].wait_recv()

    first(0)
    first(1)
    steps = NCHUNK + 5
    more_b(FRONT)
    leg(L_FRONT)
    for c in range(steps):
        for lag, act in ((5, pass_on), (4, chain_c), (3, chain_b), (2, chain_a), (1, gather_slice), (0, relay)):
            if 0 <= c - lag < NCHUNK:
                act(c - lag)
            if lag in (4, 2, 0):
                more_b(1)
        if c + 2 < NCHUNK:
            first(c + 2)
        leg(L_MID if c < NCHUNK + 5 else L_LATE)
        if c == steps - 4:
            indices()
    more_b(NB)
    more_b(NB)
    landed(0)
    leg(L_LATE)
    multiply_first()
    leg(len(legs))
    landed(1)
    have_pair(0)
    multiply_pair(0)
    have_pair(1)
    multiply_pair(1)
    for c in range(NCHUNK):
        for cp in y1s[c]:
            cp.wait_send()
        for cp in y2s[c]:
            cp.wait_send()

        @pl.when(q < NZ - 1)
        def _():
            zss[c][0].wait_send()

        @pl.when(q > 0)
        def _():
            zss[c][1].wait_send()

    @pl.when(core == 0)
    def _():
        for cp in straight[:n_even]:
            cp.wait_send()
        for cps in rounds:
            cps[0].wait_send()

    @pl.when(core == 1)
    def _():
        for cps in rounds:
            for cp in cps[1:]:
                cp.wait_send()
        for cp in straight:
            cp.wait_send()

    have_pair(2)
    multiply_pair(2)


def local(n_row, n_col, a_vals, a_cols, b_vals, b_cols, c_cols, panel_owner, atom_size):
    a = a_vals.reshape(2, ROWS, BLK)
    ac = jnp.transpose(a_cols[0, 0], (2, 0, 1))
    b = b_vals.reshape(KB * NZB, BLK, BLK)
    bc = b_cols.reshape(KB, 1, NZB)
    cc = c_cols.reshape(KB, 1, NCS)
    any_ = pl.BlockSpec(memory_space=pl.ANY)
    vmem = pl.BlockSpec(memory_space=pltpu.VMEM)
    smem = pl.BlockSpec(memory_space=pltpu.SMEM)
    bf = jnp.bfloat16
    dma = pltpu.SemaphoreType.DMA
    out, _, _ = pl.pallas_call(
        functools.partial(fox_kernel, n_row, n_col),
        out_shape=(
            jax.ShapeDtypeStruct((KB, NCS, BLK, BLK), bf),
            jax.ShapeDtypeStruct((n_col, NZA, 2, KB), jnp.int32),
            jax.ShapeDtypeStruct((KB, 1, NZB), jnp.int32),
        ),
        in_specs=[smem, smem, smem, smem, any_, any_, any_, any_],
        out_specs=(vmem, any_, any_),
        scratch_shapes=[
            pltpu.VMEM((2, ROWS, BLK), bf),
            pltpu.VMEM((2, ROWS, BLK), bf),
            pltpu.VMEM((NCHUNK, CH, BLK), bf),
            pltpu.VMEM((NCHUNK, CH, BLK), bf),
            pltpu.VMEM((NCHUNK, HF, BLK), bf),
            pltpu.VMEM((NCHUNK, HF, BLK), bf),
            pltpu.VMEM((NCHUNK, CH, BLK), bf),
            pltpu.VMEM((NCHUNK, CH, BLK), bf),
            pltpu.VMEM((NCHUNK, CH, BLK), bf),
            pltpu.VMEM((NCHUNK, CH, BLK), bf),
            pltpu.VMEM((NCHUNK, CH, BLK), bf),
            pltpu.VMEM((ROWS, BLK), bf),
            pltpu.VMEM((ROWS, BLK), bf),
            pltpu.VMEM((3, RB, BLK, BLK), bf),
            pltpu.VMEM((NB + 1, BLK, BLK), bf),
            pltpu.VMEM((NPB + 1, BLK, BLK), bf),
            pltpu.VMEM((NPB + 1, BLK, BLK), bf),
            pltpu.VMEM((NPB + 1, BLK, BLK), bf),
            pltpu.VMEM((KB, BLK, NCS * BLK), jnp.float32),
            pltpu.VMEM((BLK, NZA * BLK), bf),
            pltpu.VMEM((NZA * BLK, NCS * BLK), bf),
            pltpu.VMEM((BLK, 2 * BLK), bf),
            pltpu.VMEM((2 * BLK, NCS * BLK), bf),
            pltpu.SMEM((n_col, NZA, 2, KB), jnp.int32),
            pltpu.SMEM((KB, 1, NZB), jnp.int32),
            dma((NCHUNK, 4)), dma((NCHUNK, 4)),
            dma((NCHUNK, 2)), dma((NCHUNK, 2)),
            dma((NCHUNK, 4)), dma((NCHUNK, 4)),
            dma((NB,)), dma((NB,)),
            dma((RB, 4)), dma((RB, 4)),
            dma((n_col,)), dma((n_col,)),
            dma((5,)),
        ],
        compiler_params=pltpu.CompilerParams(collective_id=0, has_side_effects=True),
        name="fox",
    )(panel_owner, atom_size, bc, cc, a, ac, b, bc)
    return out.reshape(1, 1, KB, NCS, BLK, BLK)


def solution(mesh):
    placed = (
        P("row", "col", None, None, None, None, None),
        P("row", "col", None, None, None),
        P("row", "col", None, None, None, None),
        P("row", "col", None, None),
        P("row", "col", None, None),
        P(),
        P(),
    )
    return jax.shard_map(
        functools.partial(local, mesh.shape["row"], mesh.shape["col"]),
        mesh=mesh,
        in_specs=placed,
        out_specs=P("row", "col", None, None, None, None),
        check_vma=False,
    )
```
